128 devices in a mesh: loc: 16 (over x_hi, z, core), inc: 8 (over y, x_lo).
Axes of the slice: x: 4 (x_hi: 2, x_lo: 2; x = x_hi * 2 + x_lo), y: 4, z: 4, core: 2. Of those that a mesh axis runs over, the one named last changes fastest.
Arguments:
- cont_value: float32 [3200, 8192], P('loc', 'inc'), may hold values from -4 to 252, as said below
- flow_util: float32 [3200, 8192], P('loc', 'inc'), may hold values from -6 to 6
- move_cost: float32 [3200, 3200], P('loc'), may hold values from 0 to 6, as said below
- live_mask: int32 [3200], P('loc'), may hold values 0 or 1
- trans_weight: float32 [128, 128], replicated, may hold values from 0.02 to 1
- asset_policy: int32 [128, 64], replicated, may hold values from 0 to 63
- mass: float32 [3200, 8192], P('loc', 'inc'), may hold values from 0.1 to 1
Outputs:
- new_value: float32 [3200, 8192], P('loc', 'inc')
- new_mass: float32 [3200, 8192], P('loc', 'inc')
The draws below stay inside these ranges and needn't reach their ends.
Inputs may be any that keep to these rules, and one draw needn't show every extreme that they name: cont_value lies within the stated bounds. move_cost is symmetric with a zero diagonal; off the diagonal it lies between 0.5 and 6.
All inputs are finite; a program needn't handle non-finite values. No bound on the sum of `live_mask` on one device may be relied on, other than what follows from the above.
Results may differ from the reference program's by a relative error of at most 0.004.
Values may be sent and summed in bfloat16 or wider, within the bound.
A program may use at most 64 MiB of HBM per device.

```python
import math
import jax
import jax.numpy as jnp
from jax import lax

L = 3200
E = 128
A = 64
S = 8192


def draw_cont_value(key, part):
    key_base = jax.random.fold_in(key, 0)
    key_effect = jax.random.fold_in(key, 4)
    effect = 1.2 * jax.random.normal(key_effect, (L, 1), jnp.float32)
    noise = 0.8 * jax.random.normal(key_base, (L, E * A), jnp.float32)
    return jnp.clip(effect + noise, -4.0, 4.0)


def draw_move_cost(key, part):
    key_center, key_member, key_place = jax.random.split(key, 3)
    clusters = max(4, L // 64)
    slope, spread = (10.0, 0.05)
    centers = jax.random.uniform(key_center, (clusters, 2), jnp.float32, 0.0, 1.0)
    member = jax.random.randint(key_member, (L,), 0, clusters)
    coords = centers[member] + spread * jax.random.normal(key_place, (L, 2), jnp.float32)
    along_x = coords[:, 0][:, None] - coords[:, 0][None, :]
    along_y = coords[:, 1][:, None] - coords[:, 1][None, :]
    distance = jnp.sqrt(along_x * along_x + along_y * along_y)
    cost = jnp.clip(0.5 + slope * distance, 0.5, 6.0)
    return cost * (1.0 - jnp.eye(L, dtype=jnp.float32))


def touch_ends(values, own_key, least, largest):
    index_at = [jax.random.randint(jax.random.fold_in(own_key, axis), (), 0, length) for axis, length in enumerate(values.shape)]
    longest = values.shape.index(max(values.shape))
    next_to = index_at[:longest] + [(index_at[longest] + 1) % values.shape[longest]] + index_at[longest + 1:]
    return values.at[tuple(index_at)].set(least).at[tuple(next_to)].set(largest)


def level_of(key, dims, shards, smallest, top_value):
    loudness, own = 1.0, jax.random.fold_in(key, 6)
    for position, shards_of in shards:
        steps = jnp.exp(jax.random.uniform(jax.random.fold_in(own, position), (shards_of,), jnp.float32, smallest / len(shards), top_value / len(shards)))
        loudness = loudness * jnp.repeat(steps, dims[position] // shards_of).reshape([-1 if axis == position else 1 for axis in range(len(dims))])
    return loudness


def normal_values(own_key, shape, deviation, bound, cuts=(), held_as=jnp.bfloat16):
    loudness = level_of(own_key, shape, cuts, -0.22, 0.18) if cuts else 1.0
    result = jax.random.normal(own_key, shape, jnp.float32) * deviation * loudness
    return jnp.minimum(jnp.maximum(result, -bound), bound).astype(held_as)


def setup_inputs(seed: int = 0) -> dict:
    streams_of = jax.random.split(jax.random.key(seed), 8)
    return {
        "cont_value": draw_cont_value(jax.random.fold_in(streams_of[7], 71), 0),
        "flow_util": normal_values(streams_of[1], (L, S), 1.0, 6.0, ((0, 16), (1, 8)), jnp.float32),
        "move_cost": draw_move_cost(jax.random.fold_in(streams_of[7], 71), 0),
        "live_mask": touch_ends((jax.random.randint(streams_of[3], (L,), 0, 16) < 15).astype(jnp.int32), jax.random.fold_in(streams_of[3], 1), 0, 1),
        "trans_weight": jnp.clip(jnp.exp(jax.random.uniform(streams_of[4], (E, E), jnp.float32, math.log(0.02), math.log(1.0))), 0.02, 1.0),
        "asset_policy": touch_ends(jax.random.randint(streams_of[5], (E, A), 0, A), jax.random.fold_in(streams_of[5], 1), 0, A - 1).astype(jnp.int32),
        "mass": jnp.clip(jnp.exp(math.log(1.0) - 2.3025851 * jax.random.uniform(streams_of[6], (L, S), jnp.float32) ** level_of(streams_of[6], (L, S), ((0, 16), (1, 8)), -0.2, 0.2)), 0.1, 1.0),
    }


DISCOUNT = 0.96


def reference(cont_value, flow_util, move_cost, live_mask, trans_weight, asset_policy, mass):
    high = lax.Precision.HIGHEST
    eye_full = jnp.eye(E, dtype=jnp.float32)
    raised = trans_weight + 16.0 * eye_full
    trans_prob = raised / jnp.sum(raised, axis=1, keepdims=True)
    onehot = (asset_policy[:, :, None] == jnp.arange(A, dtype=jnp.int32)[None, None, :]).astype(jnp.float32)
    value_grid = cont_value.reshape(L, E, A)
    expect = jnp.einsum('ef,jfb->jeb', trans_prob, value_grid, precision=high)
    chosen = jnp.einsum('jeb,eab->jea', expect, onehot, precision=high).reshape(L, E * A)
    scores = DISCOUNT * chosen
    live_rows = live_mask[:, None] > 0
    column_max = jnp.max(jnp.where(live_rows, scores, jnp.float32(-1e30)), axis=0)
    dest_weight = jnp.where(live_rows, jnp.exp(scores - column_max[None, :]), jnp.float32(0.0)).astype(jnp.bfloat16)
    kernel = jnp.exp(-move_cost).astype(jnp.bfloat16)
    kernel_wide = kernel.astype(jnp.float32)
    totals = jnp.dot(kernel_wide, dest_weight.astype(jnp.float32), precision=high)
    new_value = flow_util + column_max[None, :] + jnp.log(totals)
    shares = (mass / totals).astype(jnp.bfloat16)
    arrived = jnp.dot(kernel_wide.T, shares.astype(jnp.float32), precision=high)
    movers = dest_weight.astype(jnp.float32) * arrived
    shuffled = jnp.einsum('jea,eab->jeb', movers.reshape(L, E, A), onehot, precision=high)
    new_mass = jnp.einsum('ef,jeb->jfb', trans_prob, shuffled, precision=high).reshape(L, E * A)
    return new_value, new_mass
```

```python
import functools

import jax
import jax.numpy as jnp
from jax import lax
from jax.experimental import pallas as pl
from jax.experimental.pallas import tpu as pltpu
from jax.sharding import PartitionSpec as P

E = 128
A = 64
DISCOUNT = 0.96
NEG = -1e30

MESH = pl.DeviceIdType.MESH
BF = jnp.bfloat16
F32 = jnp.float32

ROWS = 200
PAD = 208
LOC = 16
INC = 8
MINE = ROWS // INC
NC = 2
CW = 1024 // NC
TILES = 8
TPC = TILES // NC


def fold(o, lane_low):
    direct = jnp.where(lane_low, o[0:64], o[192:256])
    cross = jnp.where(lane_low, o[128:192], o[64:128])
    return direct + pltpu.roll(cross, 64, axis=1)


def split3(x):
    a = x.astype(BF)
    r = x - a.astype(F32)
    b = r.astype(BF)
    c = (r - b.astype(F32)).astype(BF)
    return a, b, c


def body(
    cont, flow, mc, live, mass, pfwd, pbwd, gidx, onehot,
    nv_out, nm_out,
    abuf, rbuf, ssend, fbuf, msend, mrecv, kp, bt, dg, ts, tr, town, xs, xr,
    shg, ao, asend, arecv, gbuf, cs, cr, ns, nf,
    lsem, s1, r1, s2, r2, sm, rm, sk, rk, sz, rz, st, rt, sx, rx, sh, rh,
    sa, ra, s3, r3, s4, r4,
):
    li = lax.axis_index("loc")
    ii = lax.axis_index("inc")
    xh = li // 8
    z = lax.rem(li // 2, 4)
    c = lax.rem(li, 2)

    def loc_of(xh_, z_, c_):
        return ((xh_ * 4 + z_) * 2 + c_, ii)

    def inc_of(d):
        return lax.rem(ii + d, INC)

    partner = loc_of(xh, z, 1 - c)
    across = loc_of(1 - xh, z, c)
    pending = []

    def send(src, dst, ssem, rsem, dev):
        cp = pltpu.make_async_remote_copy(
            src_ref=src, dst_ref=dst, send_sem=ssem, recv_sem=rsem,
            device_id=dev, device_id_type=MESH,
        )
        cp.start()
        pending.append(cp)
        return cp

    for k in range(TILES):
        abuf[pl.ds(k, ROWS, stride=8), :] = cont[:, k * 128 : (k + 1) * 128]
    shg[:, :, PAD:256, :] = jnp.zeros((NC, 4, 256 - PAD, CW), BF)

    barrier = pltpu.get_barrier_semaphore()
    for d in range(1, INC):
        pl.semaphore_signal(barrier, inc=1, device_id=(li, inc_of(d)), device_id_type=MESH)
    for d in range(1, LOC):
        pl.semaphore_signal(
            barrier, inc=1, device_id=(lax.rem(li + d, LOC), ii), device_id_type=MESH
        )
    pl.semaphore_wait(barrier, INC - 1 + LOC - 1)

    a2a = []
    for d in range(1, INC):
        peer = inc_of(d)
        a2a.append(send(
            abuf.at[pl.ds(pl.multiple_of(peer * ROWS, 8), ROWS)], rbuf.at[ii],
            s1.at[d], r1.at[d], (li, peer),
        ))
    own1 = pltpu.make_async_copy(
        abuf.at[pl.ds(pl.multiple_of(ii * ROWS, 8), ROWS)], rbuf.at[ii], lsem.at[0]
    )
    own1.start()

    for m in range(LOC):
        first = (m * ROWS) // 128 * 128
        width = 384 if first + 384 <= LOC * ROWS else 256
        shift = m * ROWS - first
        v = mc[:, first : first + width]
        if shift:
            v = pltpu.roll(v, width - shift, axis=1)
        v = jnp.exp(-v[:, :256])
        v = jnp.concatenate([v, jnp.zeros((PAD - ROWS, 256), F32)], axis=0)
        kp[(m // 2) % 4, (m // 8) * 2 + m % 2] = v.astype(BF)
    ksend = []
    for d in (2, 1, 3):
        z2 = lax.rem(z + d, 4)
        ksend.append(send(kp.at[z2], bt.at[z], sk.at[d], rk.at[d], loc_of(xh, z2, c)))
    ownk = pltpu.make_async_copy(kp.at[z], bt.at[z], lsem.at[1])
    ownk.start()

    own1.wait()
    for cp in a2a:
        cp.wait_recv()

    lane_low = lax.broadcasted_iota(jnp.int32, (64, 128), 1) < 64

    @pl.loop(0, 5)
    def _(g):
        base = pl.multiple_of(g * 40, 8)
        blk = rbuf[:, pl.ds(base, 40), :]
        cols = [blk[:, t * 8 : (t + 1) * 8, :].reshape(64, 128) for t in range(5)]
        x = jnp.concatenate(cols, axis=1)
        c1, c2, c3 = split3(x)
        stack = jnp.concatenate([c1, c1, c1, c2, c2, c3], axis=0)
        o = jnp.dot(pfwd[...], stack, preferred_element_type=F32)
        for t in range(5):
            e = fold(o[:, t * 128 : (t + 1) * 128], lane_low)
            s = jnp.take_along_axis(e, gidx[...], axis=1) * DISCOUNT
            ssend[:, pl.ds(pl.multiple_of(base + t * 8, 8), 8), :] = s.reshape(8, 8, 128)

    a2a = []
    for d in range(1, INC):
        peer = inc_of(d)
        a2a.append(send(
            ssend.at[peer], fbuf.at[pl.ds(pl.multiple_of(ii * ROWS, 8), ROWS)],
            s2.at[d], r2.at[d], (li, peer),
        ))
    own2 = pltpu.make_async_copy(
        ssend.at[ii], fbuf.at[pl.ds(pl.multiple_of(ii * ROWS, 8), ROWS)], lsem.at[2]
    )
    own2.start()
    own2.wait()
    for cp in a2a:
        cp.wait_recv()

    alive = live[...] > 0
    for k in range(TILES):
        x = fbuf[pl.ds(k, ROWS, stride=8), :]
        top = jnp.max(jnp.where(alive, x, NEG), axis=0, keepdims=True)
        msend[pl.ds(k, 1), :] = top
    maxes = []
    for d in range(1, LOC):
        maxes.append(send(
            msend, mrecv.at[li], sm.at[d], rm.at[d], (lax.rem(li + d, LOC), ii)
        ))
    ownm = pltpu.make_async_copy(msend, mrecv.at[li], lsem.at[3])
    ownm.start()
    ownm.wait()
    for cp in maxes:
        cp.wait_recv()
    cmax = jnp.max(mrecv[...], axis=0)

    zsend = {}

    def st_d(h):
        for t in range(TPC):
            k = h * TPC + t
            x = fbuf[pl.ds(k, ROWS, stride=8), :]
            w = jnp.where(alive, jnp.exp(x - cmax[k : k + 1, :]), 0.0)
            w = jnp.concatenate([w, jnp.zeros((PAD - ROWS, 128), F32)], axis=0)
            dg[h, z, :, t * 128 : (t + 1) * 128] = w.astype(BF)
        zsend[h] = [
            send(dg.at[h, z], dg.at[h, z], sz.at[h, d], rz.at[h, d],
                 loc_of(xh, lax.rem(z + d, 4), c))
            for d in (2, 1, 3)
        ]

    tsend = {}

    def st_mm1(h):
        if h == 0:
            ownk.wait()
            for cp in ksend:
                cp.wait_recv()
        for cp in zsend[h]:
            cp.wait_recv()
        dall = dg[h].reshape(4 * PAD, CW)
        for mine in (False, True):
            for x2 in range(2):
                p = x2 * 2 + (c if mine else 1 - c)
                lhs = bt[:, p].reshape(4 * PAD, 256)
                t = lax.dot_general(
                    lhs, dall, (((0,), (0,)), ((), ())), preferred_element_type=F32
                )[:PAD]
                if mine:
                    town[h, x2] = t
                else:
                    ts[h, x2] = t.astype(BF)
            if not mine:
                tsend[h] = send(ts.at[h], tr.at[h], st.at[h], rt.at[h], partner)

    xsend = {}

    def st_x(h):
        tsend[h].wait_recv()
        xs[h] = (town[h, 1 - xh] + tr[h, 1 - xh].astype(F32)).astype(BF)
        xsend[h] = send(xs.at[h], xr.at[h], sx.at[h], rx.at[h], across)

    hsend = {}

    def st_share(h):
        xsend[h].wait_recv()
        cols = slice(h * CW, (h + 1) * CW)
        tot = town[h, xh] + tr[h, xh].astype(F32) + xr[h].astype(F32)
        tot = tot[:ROWS]
        lt = jnp.log(tot)
        for t in range(TPC):
            k = h * TPC + t
            wide = slice(k * 128, (k + 1) * 128)
            nv_out[:, wide] = flow[:, wide] + cmax[k : k + 1, :] + lt[:, t * 128 : (t + 1) * 128]
        sv = mass[:, cols] / tot
        sv = jnp.concatenate([sv, jnp.zeros((PAD - ROWS, CW), F32)], axis=0)
        p = xh * 2 + c
        shg[h, p, 0:PAD, :] = sv.astype(BF)
        ref = shg.at[h, p, pl.ds(0, PAD)]
        hsend[h] = [
            send(ref, ref, sh.at[h, 0], rh.at[h, 0], across),
            send(ref, ref, sh.at[h, 1], rh.at[h, 1], partner),
        ]

    def st_fwd(h):
        hsend[h][0].wait_recv()
        ref = shg.at[h, (1 - xh) * 2 + c, pl.ds(0, PAD)]
        hsend[h].append(send(ref, ref, sh.at[h, 2], rh.at[h, 2], partner))

    asends = {}

    def st_mm2(h):
        hsend[h][1].wait_recv()
        hsend[h][2].wait_recv()
        sall = shg[h].reshape(4 * 256, CW)
        asends[h] = []
        for d in (2, 1, 3, 0):
            q = lax.rem(z + d, 4)
            lhs = jnp.concatenate([bt[q, p] for p in range(4)], axis=1)
            a = jnp.dot(lhs, sall, preferred_element_type=F32)
            if d == 0:
                ao[h] = a
            else:
                asend[h, d - 1] = a.astype(BF)
                asends[h].append(send(
                    asend.at[h, d - 1], arecv.at[h, d - 1], sa.at[h, d], ra.at[h, d],
                    loc_of(xh, q, c),
                ))

    def st_move(h):
        for cp in asends[h]:
            cp.wait_recv()
        for t in range(TPC):
            k = h * TPC + t
            lanes = slice(t * 128, (t + 1) * 128)
            arrived = ao[h, :, lanes] + arecv[h, 0, :, lanes].astype(F32)
            arrived = arrived + arecv[h, 1, :, lanes].astype(F32)
            arrived = arrived + arecv[h, 2, :, lanes].astype(F32)
            mv = dg[h, z, :, lanes].astype(F32) * arrived
            hi = mv.astype(BF)
            lo = (mv - hi.astype(F32)).astype(BF)
            sf = jnp.dot(hi, onehot[k], preferred_element_type=F32)
            sf = sf + jnp.dot(lo, onehot[k], preferred_element_type=F32)
            gbuf[pl.ds(k, ROWS, stride=8), :] = sf[:ROWS]

    stages = [st_d, st_mm1, st_x, st_share, st_fwd, st_mm2, st_move]
    for step in range(NC + len(stages) - 1):
        for s in reversed(range(len(stages))):
            if 0 <= step - s < NC:
                stages[s](step - s)

    for i in range(INC):
        blk = gbuf[i * ROWS : (i + 1) * ROWS, :]
        blk = jnp.concatenate([blk, jnp.zeros((PAD - ROWS, 128), F32)], axis=0)
        cs[i] = blk.astype(BF)
    a2a = []
    for d in range(1, INC):
        peer = inc_of(d)
        a2a.append(send(cs.at[peer], cr.at[ii], s3.at[d], r3.at[d], (li, peer)))
    own3 = pltpu.make_async_copy(cs.at[ii], cr.at[ii], lsem.at[4])
    own3.start()
    own3.wait()
    for cp in a2a:
        cp.wait_recv()

    @pl.loop(0, PAD // 16)
    def _(g):
        base = pl.multiple_of(g * 16, 16)
        blk = cr[:, pl.ds(base, 16), :].astype(F32)
        x = jnp.concatenate(
            [blk[:, t * 8 : (t + 1) * 8, :].reshape(64, 128) for t in range(2)], axis=1
        ).astype(BF)
        stack = jnp.concatenate([x, x, x], axis=0)
        o = jnp.dot(pbwd[...], stack, preferred_element_type=F32)
        for t in range(2):
            e = fold(o[:, t * 128 : (t + 1) * 128], lane_low)
            ns[:, pl.ds(pl.multiple_of(base + t * 8, 8), 8), :] = e.reshape(8, 8, 128)

    a2a = []
    for d in range(1, INC):
        peer = inc_of(d)
        a2a.append(send(
            ns.at[peer, pl.ds(0, ROWS)], nf.at[pl.ds(pl.multiple_of(ii * ROWS, 8), ROWS)],
            s4.at[d], r4.at[d], (li, peer),
        ))
    own4 = pltpu.make_async_copy(
        ns.at[ii, pl.ds(0, ROWS)], nf.at[pl.ds(pl.multiple_of(ii * ROWS, 8), ROWS)], lsem.at[5]
    )
    own4.start()
    own4.wait()
    for cp in a2a:
        cp.wait_recv()
    for k in range(TILES):
        nm_out[:, k * 128 : (k + 1) * 128] = nf[pl.ds(k, ROWS, stride=8), :]
    for cp in pending:
        cp.wait_send()


def shards(cont_value, flow_util, move_cost, live_mask, trans_weight, asset_policy, mass):
    raised = trans_weight + 16.0 * jnp.eye(E, dtype=F32)
    prob = raised / jnp.sum(raised, axis=1, keepdims=True)
    four = prob.reshape(64, 2, 64, 2)
    fwd = four.transpose(1, 3, 0, 2).reshape(256, 64)
    bwd = four.transpose(3, 1, 2, 0).reshape(256, 64)
    f1, f2, f3 = split3(fwd)
    b1, b2, b3 = split3(bwd)
    pfwd = jnp.concatenate([f1, f2, f3, f1, f2, f1], axis=1)
    pbwd = jnp.concatenate([b1, b2, b3], axis=1)
    half = (jnp.arange(128, dtype=jnp.int32) // 64) * 64
    gidx = asset_policy.reshape(64, 128) + half[None, :]
    own = lax.dynamic_slice_in_dim(gidx, lax.axis_index("inc") * TILES, TILES, 0)
    onehot = (own[:, :, None] == jnp.arange(128, dtype=jnp.int32)[None, None, :]).astype(BF)
    live = jnp.broadcast_to(live_mask[:, None], (ROWS, 128))

    vm = pl.BlockSpec(memory_space=pltpu.VMEM)
    dma = pltpu.SemaphoreType.DMA
    out = jax.ShapeDtypeStruct((ROWS, 1024), F32)
    return pl.pallas_call(
        body,
        out_shape=(out, out),
        in_specs=[vm] * 9,
        out_specs=(vm, vm),
        scratch_shapes=[
            pltpu.VMEM((8 * ROWS, 128), F32),
            pltpu.VMEM((INC, ROWS, 128), F32),
            pltpu.VMEM((INC, ROWS, 128), F32),
            pltpu.VMEM((8 * ROWS, 128), F32),
            pltpu.VMEM((8, 128), F32),
            pltpu.VMEM((LOC, 8, 128), F32),
            pltpu.VMEM((4, 4, PAD, 256), BF),
            pltpu.VMEM((4, 4, PAD, 256), BF),
            pltpu.VMEM((NC, 4, PAD, CW), BF),
            pltpu.VMEM((NC, 2, PAD, CW), BF),
            pltpu.VMEM((NC, 2, PAD, CW), BF),
            pltpu.VMEM((NC, 2, PAD, CW), F32),
            pltpu.VMEM((NC, PAD, CW), BF),
            pltpu.VMEM((NC, PAD, CW), BF),
            pltpu.VMEM((NC, 4, 256, CW), BF),
            pltpu.VMEM((NC, PAD, CW), F32),
            pltpu.VMEM((NC, 3, PAD, CW), BF),
            pltpu.VMEM((NC, 3, PAD, CW), BF),
            pltpu.VMEM((8 * ROWS, 128), F32),
            pltpu.VMEM((INC, PAD, 128), BF),
            pltpu.VMEM((INC, PAD, 128), BF),
            pltpu.VMEM((INC, PAD, 128), F32),
            pltpu.VMEM((8 * ROWS, 128), F32),
            dma((6,)),
            dma((8,)), dma((8,)), dma((8,)), dma((8,)),
            dma((16,)), dma((16,)), dma((4,)), dma((4,)),
            dma((NC, 4)), dma((NC, 4)), dma((NC,)), dma((NC,)),
            dma((NC,)), dma((NC,)), dma((NC, 3)), dma((NC, 3)),
            dma((NC, 4)), dma((NC, 4)),
            dma((8,)), dma((8,)), dma((8,)), dma((8,)),
        ],
        compiler_params=pltpu.CompilerParams(
            collective_id=0, has_side_effects=True, vmem_limit_bytes=60 * 1024 * 1024
        ),
        name="county_step",
    )(cont_value, flow_util, move_cost, live, mass, pfwd, pbwd, gidx, onehot)


def solution(mesh):
    return jax.shard_map(
        shards,
        mesh=mesh,
        in_specs=(
            P("loc", "inc"),
            P("loc", "inc"),
            P("loc", None),
            P("loc"),
            P(),
            P(),
            P("loc", "inc"),
        ),
        out_specs=(P("loc", "inc"), P("loc", "inc")),
        check_vma=False,
    )
```

```python
import jax
import jax.numpy as jnp
from jax import lax
from jax.experimental import pallas as pl
from jax.experimental.pallas import tpu as pltpu
from jax.sharding import PartitionSpec as P

E = 128
A = 64
DISCOUNT = 0.96
DEAD = 1e30

MESH = pl.DeviceIdType.MESH
BF = jnp.bfloat16
F32 = jnp.float32

ROWS = 200
INC = 8
MINE = ROWS // INC
PLANE = 16
L = 3200
NC = 2
TPC = 4 // NC
CW = TPC * 128
PIECE = TPC * MINE


def fold(o, lane_low):
    direct = jnp.where(lane_low, o[0:64], o[192:256])
    cross = jnp.where(lane_low, o[128:192], o[64:128])
    return direct + pltpu.roll(cross, 64, axis=1)


def split3(x):
    a = x.astype(BF)
    r = x - a.astype(F32)
    b = r.astype(BF)
    c = (r - b.astype(F32)).astype(BF)
    return a, b, c


def body(
    cont_h, mc_h, mass_h, live, tw, pol,
    v_out, nm_out,
    cont, mc, mass,
    abuf, rbuf, sb, ssend, msd, mrv, mds, mdr, fb, fc, kp, dall, shall, mz, msnd,
    tots, vsend, sfr, csf, cs, cr, xf, ns,
    pscr, ptscr, pfwd, pbwd, onehot,
    lsem, s1, r1, s2, r2, sm, rm, sd, rd, sk, rk, sg, rg, sv, rv, s3, r3, s4, r4,
):
    li = lax.axis_index("loc")
    ii = lax.axis_index("inc")
    xh = li // 8
    z = lax.rem(li // 2, 4)
    c = lax.rem(li, 2)
    g = ii * 2 + xh
    slot = xh * 8 + ii
    blk = z * 2 + c

    def dev(xh_, z_, c_, ii_):
        return ((xh_ * 4 + z_) * 2 + c_, ii_)

    up = lax.rem(z + 1, 4)
    down = lax.rem(z + 3, 4)
    far = lax.rem(z + 2, 4)
    partner = dev(xh, z, 1 - c, ii)
    across = dev(1 - xh, z, c, ii)
    pending = []

    def send(src, dst, ssem, rsem, to):
        cp = pltpu.make_async_remote_copy(
            src_ref=src, dst_ref=dst, send_sem=ssem, recv_sem=rsem,
            device_id=to, device_id_type=MESH,
        )
        cp.start()
        pending.append(cp)
        return cp

    def local(src, dst, k):
        cp = pltpu.make_async_copy(src, dst, lsem.at[k])
        cp.start()
        return cp

    in1 = local(cont_h, cont, 0)
    in2 = local(mc_h, mc, 1)
    in3 = local(mass_h, mass, 2)

    barrier = pltpu.get_barrier_semaphore()
    plane = []
    for d in range(1, PLANE):
        g2 = lax.rem(g + d, PLANE)
        plane.append((g2, dev(lax.rem(g2, 2), z, c, g2 // 2), lax.rem(g2, 2) * 8 + g2 // 2))
    column = []
    for d in range(1, 8):
        b2 = lax.rem(blk + d, 8)
        column.append(dev(xh, b2 // 2, lax.rem(b2, 2), ii))
    for _, to, _ in plane:
        pl.semaphore_signal(barrier, inc=1, device_id=to, device_id_type=MESH)
    for to in column:
        pl.semaphore_signal(barrier, inc=1, device_id=to, device_id_type=MESH)

    in1.wait()
    for k in range(8):
        abuf[pl.ds(k, ROWS, stride=8), :] = cont[:, k * 128 : (k + 1) * 128]
    pl.semaphore_wait(barrier, PLANE - 1 + 7)

    a2a = []
    for d in range(1, INC):
        peer = lax.rem(ii + d, INC)
        a2a.append(send(
            abuf.at[pl.ds(pl.multiple_of(peer * ROWS, 8), ROWS)], rbuf.at[ii],
            s1.at[d], r1.at[d], (li, peer),
        ))
    own1 = local(abuf.at[pl.ds(pl.multiple_of(ii * ROWS, 8), ROWS)], rbuf.at[ii], 3)

    in2.wait()
    for x2 in range(2):
        for b in range(8):
            src = (x2 * 8 + b) * ROWS
            dst = (b * 2 + x2) * ROWS
            kp[xh, :, dst : dst + ROWS] = jnp.exp(-mc[:, src : src + ROWS]).astype(BF)
    ksend = send(kp.at[xh], kp.at[xh], sk.at[0], rk.at[0], across)

    in3.wait()
    mz[xh] = mass[:, pl.ds(pl.multiple_of(xh * 512, 512), 512)].astype(BF)
    msnd[...] = mass[:, pl.ds(pl.multiple_of((1 - xh) * 512, 512), 512)].astype(BF)
    msend = send(msnd, mz.at[xh], sk.at[1], rk.at[1], across)

    row = lax.broadcasted_iota(jnp.int32, (128, 128), 0)
    col = lax.broadcasted_iota(jnp.int32, (128, 128), 1)
    raised = tw[...] + jnp.where(row == col, 16.0, 0.0)
    prob = raised / jnp.sum(raised, axis=1, keepdims=True)
    pscr[...] = prob
    ptscr[...] = prob.T

    def pick(parity, high):
        want = col - 64 if high else col
        keep = (want >= 0) & (want < 64) & (row == 2 * want + parity)
        return jnp.where(keep, 1.0, 0.0).astype(BF)

    for scr, out, pairs in (
        (pscr, pfwd, ((0, 1), (2, 0), (1, 0))),
        (ptscr, pbwd, ((0, 1), (2, None))),
    ):
        for po in range(2):
            parts = split3(scr[pl.ds(po, 64, stride=2), :])
            for pi in range(2):
                low, high = pick(pi, False), pick(pi, True)
                for n, (a, b) in enumerate(pairs):
                    q = jnp.dot(parts[a], low, preferred_element_type=F32)
                    if b is not None:
                        q = q + jnp.dot(parts[b], high, preferred_element_type=F32)
                    r0 = (po * 2 + pi) * 64
                    out[r0 : r0 + 64, n * 128 : (n + 1) * 128] = q.astype(BF)

    lane64 = lax.broadcasted_iota(jnp.int32, (64, 128), 1)
    lane_low = lane64 < 64
    gidx = pol[...] + jnp.where(lane_low, 0, 64)
    gown = pol[pl.ds(g * 4, 4), :] + jnp.where(col[0:4] < 64, 0, 64)
    for t in range(4):
        wide = jnp.broadcast_to(gown[t : t + 1].astype(F32), (128, 128)).T
        onehot[t] = jnp.where(wide == col.astype(F32), 1.0, 0.0).astype(BF)

    own1.wait()
    for cp in a2a:
        cp.wait_recv()

    def mix(i, top):
        base = pl.multiple_of(i * 40, 8)
        piece = rbuf[:, pl.ds(base, 40), :]
        cols = [piece[:, t * 8 : (t + 1) * 8, :].reshape(64, 128) for t in range(5)]
        c1, c2, c3 = split3(jnp.concatenate(cols, axis=1))
        stack = jnp.concatenate([c1, c1, c1, c2, c2, c3], axis=0)
        o = jnp.dot(pfwd[...], stack, preferred_element_type=F32)
        for t in range(5):
            e = fold(o[:, t * 128 : (t + 1) * 128], lane_low)
            s = jnp.take_along_axis(e, gidx, axis=1) * DISCOUNT
            alive = live[ii * MINE + i * 5 + t].astype(F32)
            s = s + (alive - 1.0) * DEAD
            top = jnp.maximum(top, s)
            sb[pl.ds(pl.multiple_of((i * 5 + t) * 64, 64), 64), :] = s
        return top

    top = lax.fori_loop(0, 5, mix, jnp.full((64, 128), -2 * DEAD, F32))
    for k in range(PLANE):
        msd[k] = top[k * 4 : (k + 1) * 4]
    tops = [
        send(msd.at[g2], mrv.at[slot], sm.at[d + 1], rm.at[d + 1], to)
        for d, (g2, to, _) in enumerate(plane)
    ]
    ownm = local(msd.at[g], mrv.at[slot], 4)
    scat = {}
    owns = {}
    for h in range(NC):
        for k in range(PLANE):
            for t in range(TPC):
                tile = k * 4 + h * TPC + t
                ssend[h, k, t * MINE : (t + 1) * MINE, :] = sb[pl.ds(tile, MINE, stride=64), :]
        scat[h] = [
            send(ssend.at[h, g2], fb.at[h, slot], s2.at[h, d + 1], r2.at[h, d + 1], to)
            for d, (g2, to, _) in enumerate(plane)
        ]
        owns[h] = local(ssend.at[h, g], fb.at[h, slot], 5 + h)

    ownm.wait()
    for cp in tops:
        cp.wait_recv()
    mds[...] = jnp.max(mrv[...], axis=0)
    maxes = [
        send(mds, mdr.at[blk], sd.at[d + 1], rd.at[d + 1], to)
        for d, to in enumerate(column)
    ]
    mdr[blk] = mds[...]
    for cp in maxes:
        cp.wait_recv()
    cmax = jnp.max(mdr[...], axis=0)

    my_rows = pl.ds(pl.multiple_of(blk * 400, 16), 400)

    def rows_of(z_, c_):
        return pl.ds(pl.multiple_of((z_ * 2 + c_) * 400, 16), 400)

    got = {}

    def gather0(n, buf, h):
        ref = buf.at[h, my_rows]
        got[n, h] = [
            send(ref, ref, sg.at[n, h, 0], rg.at[n, h, 0], dev(xh, up, c, ii)),
            send(ref, ref, sg.at[n, h, 1], rg.at[n, h, 1], dev(xh, down, c, ii)),
            send(ref, ref, sg.at[n, h, 2], rg.at[n, h, 2], partner),
        ]

    def gather1(n, buf, h):
        w = got[n, h]
        for k, (src, to) in enumerate(((down, up), (up, down))):
            w[k].wait_recv()
            half = buf.at[h, rows_of(src, c), pl.ds(k * (CW // 2), CW // 2)]
            w.append(send(half, half, sg.at[n, h, 3 + k], rg.at[n, h, 3 + k], dev(xh, to, c, ii)))
            ref = buf.at[h, rows_of(src, c)]
            w.append(send(ref, ref, sg.at[n, h, 5 + k], rg.at[n, h, 5 + k], partner))

    def gather2(n, buf, h):
        w = got[n, h]
        for k, cp in enumerate((w[3], w[5])):
            cp.wait_recv()
            half = buf.at[h, rows_of(far, c), pl.ds(k * (CW // 2), CW // 2)]
            w.append(send(half, half, sg.at[n, h, 7 + k], rg.at[n, h, 7 + k], partner))

    def gather3(n, buf, h):
        w = got[n, h]
        for cp in (w[2], w[4], w[6], w[7], w[8]):
            cp.wait_recv()

    def st_d(h):
        owns[h].wait()
        for cp in scat[h]:
            cp.wait_recv()
        for t in range(TPC):
            for k in range(PLANE):
                fc[k * MINE : (k + 1) * MINE, t * 128 : (t + 1) * 128] = fb[
                    h, k, t * MINE : (t + 1) * MINE, :
                ]
        for t in range(TPC):
            k = h * TPC + t
            lanes = slice(t * 128, (t + 1) * 128)
            dall[h, my_rows, lanes] = jnp.exp(fc[:, lanes] - cmax[k : k + 1, :]).astype(BF)
        gather0(0, dall, h)

    def st_share(h):
        gather3(0, dall, h)
        if h == 0:
            ksend.wait_recv()
            msend.wait_recv()
        for x2 in range(2):
            tots[x2] = jnp.dot(kp[x2], dall[h], preferred_element_type=F32)
        sh = []
        for x2 in range(2):
            sh.append(mz[x2, :, h * CW : (h + 1) * CW].astype(F32) / tots[x2])
        shall[h, my_rows, :] = jnp.concatenate(sh, axis=0).astype(BF)
        gather0(1, shall, h)
        cm = jnp.concatenate([cmax[h * TPC + t : h * TPC + t + 1, :] for t in range(TPC)], axis=1)
        cols = pl.ds(pl.multiple_of(xh * 512 + h * CW, 128), CW)
        v_out[:, cols] = cm + jnp.log(tots[xh])
        vsend[h] = cm + jnp.log(tots[1 - xh])
        vs.append(send(vsend.at[h], v_out.at[:, cols], sv.at[h], rv.at[h], across))

    vs = []
    back = {}
    ownb = {}

    def st_move(h):
        gather3(1, shall, h)
        for x2 in range(2):
            tots[x2] = jnp.dot(kp[x2], shall[h], preferred_element_type=F32)
        arrived = jnp.concatenate([tots[0], tots[1]], axis=0)
        for t in range(TPC):
            lanes = slice(t * 128, (t + 1) * 128)
            mv = dall[h, my_rows, lanes].astype(F32) * arrived[:, lanes]
            hi = mv.astype(BF)
            lo = (mv - hi.astype(F32)).astype(BF)
            oh = onehot[h * TPC + t]
            sfr[...] = jnp.dot(hi, oh, preferred_element_type=F32) + jnp.dot(
                lo, oh, preferred_element_type=F32
            )
            for k in range(PLANE):
                csf[k, t * MINE : (t + 1) * MINE, :] = sfr[k * MINE : (k + 1) * MINE, :]
        for k in range(PLANE):
            cs[h, k] = csf[k].astype(BF)
        back[h] = [
            send(cs.at[h, s2_], cr.at[h, g], s3.at[h, d + 1], r3.at[h, d + 1], to)
            for d, (_, to, s2_) in enumerate(plane)
        ]
        ownb[h] = local(cs.at[h, slot], cr.at[h, g], 5 + NC + h)

    stages = [
        st_d,
        lambda h: gather1(0, dall, h),
        lambda h: gather2(0, dall, h),
        st_share,
        lambda h: gather1(1, shall, h),
        lambda h: gather2(1, shall, h),
        st_move,
    ]
    for step in range(NC + len(stages) - 1):
        for s in reversed(range(len(stages))):
            if 0 <= step - s < NC:
                stages[s](step - s)

    for h in range(NC):
        ownb[h].wait()
        for cp in back[h]:
            cp.wait_recv()
        for k in range(PLANE):
            first = k * 4 * MINE + h * PIECE
            xf[first : first + PIECE, :] = cr[h, k].astype(F32)

    @pl.loop(0, 5)
    def _(i):
        x = jnp.concatenate(
            [xf[pl.ds(i * 5 + t, 64, stride=MINE), :] for t in range(5)], axis=1
        ).astype(BF)
        stack = jnp.concatenate([x, x, x, x], axis=0)
        o = jnp.dot(pbwd[...], stack, preferred_element_type=F32)
        for t in range(5):
            e = fold(o[:, t * 128 : (t + 1) * 128], lane_low)
            ns[:, pl.ds(pl.multiple_of(i * 40 + t * 8, 8), 8), :] = e.reshape(8, 8, 128)

    mine = pl.ds(pl.multiple_of(ii * ROWS, 8), ROWS)
    a2a = []
    for d in range(1, INC):
        peer = lax.rem(ii + d, INC)
        a2a.append(send(ns.at[peer], nm_out.at[mine], s4.at[d], r4.at[d], (li, peer)))
    own4 = local(ns.at[ii], nm_out.at[mine], 5 + 2 * NC)
    own4.wait()
    for cp in a2a:
        cp.wait_recv()
    for cp in vs:
        cp.wait_recv()
    for cp in pending:
        cp.wait_send()


def shards(cont_value, flow_util, move_cost, live_mask, trans_weight, asset_policy, mass):
    vm = pl.BlockSpec(memory_space=pltpu.VMEM)
    any_ = pl.BlockSpec(memory_space=pl.ANY)
    dma = pltpu.SemaphoreType.DMA
    v, nm = pl.pallas_call(
        body,
        out_shape=(
            jax.ShapeDtypeStruct((ROWS, 1024), F32),
            jax.ShapeDtypeStruct((8 * ROWS, 128), F32),
        ),
        in_specs=[any_, any_, any_, pl.BlockSpec(memory_space=pltpu.SMEM), vm, vm],
        out_specs=(vm, vm),
        scratch_shapes=[
            pltpu.VMEM((ROWS, 1024), F32),
            pltpu.VMEM((ROWS, L), F32),
            pltpu.VMEM((ROWS, 1024), F32),
            pltpu.VMEM((8 * ROWS, 128), F32),
            pltpu.VMEM((INC, ROWS, 128), F32),
            pltpu.VMEM((MINE * 64, 128), F32),
            pltpu.VMEM((NC, PLANE, PIECE, 128), F32),
            pltpu.VMEM((PLANE, 4, 128), F32),
            pltpu.VMEM((PLANE, 4, 128), F32),
            pltpu.VMEM((4, 128), F32),
            pltpu.VMEM((8, 4, 128), F32),
            pltpu.VMEM((NC, PLANE, PIECE, 128), F32),
            pltpu.VMEM((2 * ROWS, CW), F32),
            pltpu.VMEM((2, ROWS, L), BF),
            pltpu.VMEM((NC, L, CW), BF),
            pltpu.VMEM((NC, L, CW), BF),
            pltpu.VMEM((2, ROWS, 512), BF),
            pltpu.VMEM((ROWS, 512), BF),
            pltpu.VMEM((2, ROWS, CW), F32),
            pltpu.VMEM((NC, ROWS, CW), F32),
            pltpu.VMEM((2 * ROWS, 128), F32),
            pltpu.VMEM((PLANE, PIECE, 128), F32),
            pltpu.VMEM((NC, PLANE, PIECE, 128), BF),
            pltpu.VMEM((NC, PLANE, PIECE, 128), BF),
            pltpu.VMEM((MINE * 64, 128), F32),
            pltpu.VMEM((INC, ROWS, 128), F32),
            pltpu.VMEM((128, 128), F32),
            pltpu.VMEM((128, 128), F32),
            pltpu.VMEM((256, 384), BF),
            pltpu.VMEM((256, 256), BF),
            pltpu.VMEM((4, 128, 128), BF),
            dma((6 + 2 * NC,)),
            dma((8,)), dma((8,)), dma((NC, 16)), dma((NC, 16)),
            dma((16,)), dma((16,)), dma((8,)), dma((8,)),
            dma((2,)), dma((2,)), dma((2, NC, 9)), dma((2, NC, 9)),
            dma((NC,)), dma((NC,)), dma((NC, 16)), dma((NC, 16)),
            dma((8,)), dma((8,)),
        ],
        compiler_params=pltpu.CompilerParams(
            collective_id=0, has_side_effects=True, vmem_limit_bytes=60 * 1024 * 1024
        ),
        name="county_step",
    )(cont_value, move_cost, mass, live_mask, trans_weight, asset_policy.reshape(64, 128))
    return flow_util + v, nm.reshape(ROWS, 1024)


def solution(mesh):
    return jax.shard_map(
        shards,
        mesh=mesh,
        in_specs=(
            P("loc", "inc"),
            P("loc", "inc"),
            P("loc", None),
            P("loc"),
            P(),
            P(),
            P("loc", "inc"),
        ),
        out_specs=(P("loc", "inc"), P("loc", "inc")),
        check_vma=False,
    )
```

```python
import jax
import jax.numpy as jnp
from jax import lax
from jax.experimental import pallas as pl
from jax.experimental.pallas import tpu as pltpu
from jax.sharding import PartitionSpec as P

E = 128
A = 64
DISCOUNT = 0.96
DEAD = 1e30

MESH = pl.DeviceIdType.MESH
BF = jnp.bfloat16
F32 = jnp.float32

ROWS = 200
INC = 8
MINE = ROWS // INC
PLANE = 16
L = 3200
NC = 2
TPC = 4 // NC
CW = TPC * 128
PIECE = TPC * MINE


def fold(o, lane_low):
    direct = jnp.where(lane_low, o[0:64], o[192:256])
    cross = jnp.where(lane_low, o[128:192], o[64:128])
    return direct + pltpu.roll(cross, 64, axis=1)


def split3(x):
    a = x.astype(BF)
    r = x - a.astype(F32)
    b = r.astype(BF)
    c = (r - b.astype(F32)).astype(BF)
    return a, b, c


def body(
    cont_h, mc_h, mass_h, live, tw, pol,
    v_out, nm_out,
    cont, mc, mass,
    ko, kt, kr, abuf, rbuf, sb, ssend, msd, mrv, mds, mdr, fb, fc, kp, dall, shall, mz, msnd,
    tots, vown, vsend, sfr, csf, cs, cr, xf, ns,
    gsc, pscr, ptscr, pfwd, pbwd, onehot,
    lsem, s1, r1, s2, r2, sm, rm, sd, rd, sk, rk, sg, rg, sv, rv, s3, r3, s4, r4,
):
    li = lax.axis_index("loc")
    ii = lax.axis_index("inc")
    xh = li // 8
    z = lax.rem(li // 2, 4)
    c = lax.rem(li, 2)
    g = ii * 2 + xh
    slot = xh * 8 + ii
    blk = z * 2 + c

    def dev(xh_, z_, c_, ii_):
        return ((xh_ * 4 + z_) * 2 + c_, ii_)

    up = lax.rem(z + 1, 4)
    down = lax.rem(z + 3, 4)
    far = lax.rem(z + 2, 4)
    partner = dev(xh, z, 1 - c, ii)
    across = dev(1 - xh, z, c, ii)
    pending = []

    def send(src, dst, ssem, rsem, to):
        cp = pltpu.make_async_remote_copy(
            src_ref=src, dst_ref=dst, send_sem=ssem, recv_sem=rsem,
            device_id=to, device_id_type=MESH,
        )
        cp.start()
        pending.append(cp)
        return cp

    def local(src, dst, k):
        cp = pltpu.make_async_copy(src, dst, lsem.at[k])
        cp.start()
        return cp

    in1 = local(cont_h, cont, 0)
    in2 = local(mc_h, mc, 1)
    in3 = local(mass_h, mass, 2)

    barrier = pltpu.get_barrier_semaphore()
    plane = []
    for d in range(1, PLANE):
        g2 = lax.rem(g + d, PLANE)
        plane.append((g2, dev(lax.rem(g2, 2), z, c, g2 // 2), lax.rem(g2, 2) * 8 + g2 // 2))
    column = []
    for d in range(1, 8):
        b2 = lax.rem(blk + d, 8)
        column.append(dev(xh, b2 // 2, lax.rem(b2, 2), ii))
    for _, to, _ in plane:
        pl.semaphore_signal(barrier, inc=1, device_id=to, device_id_type=MESH)
    for to in column:
        pl.semaphore_signal(barrier, inc=1, device_id=to, device_id_type=MESH)

    in1.wait()
    for k in range(8):
        abuf[pl.ds(k, ROWS, stride=8), :] = cont[:, k * 128 : (k + 1) * 128]
    in2.wait()
    for x2 in range(2):

        @pl.when(xh == x2)
        def _():
            for b in range(8):
                src = (x2 * 8 + b) * ROWS
                ko[b] = jnp.exp(-mc[:, src : src + ROWS]).astype(BF)

    pl.semaphore_wait(barrier, PLANE - 1 + 7)
    beside = dev(1 - xh, z, c, ii + 1 - 2 * lax.rem(ii, 2))
    ksend = [send(ko, kr.at[xh], sk.at[0], rk.at[0], beside)]

    a2a = []
    for d in range(1, INC):
        peer = lax.rem(ii + d, INC)
        a2a.append(send(
            abuf.at[pl.ds(pl.multiple_of(peer * ROWS, 8), ROWS)], rbuf.at[ii],
            s1.at[d], r1.at[d], (li, peer),
        ))
    own1 = local(abuf.at[pl.ds(pl.multiple_of(ii * ROWS, 8), ROWS)], rbuf.at[ii], 3)

    for x2 in range(2):
        for b in range(8):
            src = (x2 * 8 + b) * ROWS
            dst = (b * 2 + x2) * ROWS
            kp[xh, :, dst : dst + ROWS] = jnp.exp(-mc[:, src : src + ROWS]).astype(BF)

        @pl.when(xh != x2)
        def _():
            for b in range(8):
                src = (x2 * 8 + b) * ROWS
                kt[b] = jnp.exp(-mc[:, src : src + ROWS]).T.astype(BF)

    for d, to in enumerate(column):
        b2 = lax.rem(blk + d + 1, 8)
        ksend.append(send(kt.at[b2], kr.at[xh, blk], sk.at[2 + d], rk.at[2 + d], to))
    ownk = local(kt.at[blk], kr.at[xh, blk], 6 + 2 * NC)

    row = lax.broadcasted_iota(jnp.int32, (128, 128), 0)
    col = lax.broadcasted_iota(jnp.int32, (128, 128), 1)
    raised = tw[...] + jnp.where(row == col, 16.0, 0.0)
    prob = raised / jnp.sum(raised, axis=1, keepdims=True)
    pscr[...] = prob
    ptscr[...] = prob.T

    def pick(parity, high):
        want = col - 64 if high else col
        keep = (want >= 0) & (want < 64) & (row == 2 * want + parity)
        return jnp.where(keep, 1.0, 0.0).astype(BF)

    for scr, out, pairs in (
        (pscr, pfwd, ((0, 1), (2, 0), (1, 0))),
        (ptscr, pbwd, ((0, 1), (2, None))),
    ):
        for po in range(2):
            parts = split3(scr[pl.ds(po, 64, stride=2), :])
            for pi in range(2):
                low, high = pick(pi, False), pick(pi, True)
                for n, (a, b) in enumerate(pairs):
                    q = jnp.dot(parts[a], low, preferred_element_type=F32)
                    if b is not None:
                        q = q + jnp.dot(parts[b], high, preferred_element_type=F32)
                    r0 = (po * 2 + pi) * 64
                    out[r0 : r0 + 64, n * 128 : (n + 1) * 128] = q.astype(BF)

    lane64 = lax.broadcasted_iota(jnp.int32, (64, 128), 1)
    lane_low = lane64 < 64
    gsc[...] = jnp.concatenate(
        [pol[pl.ds(0, 64, stride=2), :], pol[pl.ds(1, 64, stride=2), :] + 64], axis=1
    )
    gidx = gsc[...]
    gown = gsc[pl.ds(g * 4, 4), :]
    for t in range(4):
        wide = jnp.broadcast_to(gown[t : t + 1].astype(F32), (128, 128)).T
        onehot[t] = jnp.where(wide == col.astype(F32), 1.0, 0.0).astype(BF)

    own1.wait()
    for cp in a2a:
        cp.wait_recv()

    def mix(i, top):
        base = pl.multiple_of(i * 40, 8)
        piece = rbuf[:, pl.ds(base, 40), :]
        cols = [piece[:, t * 8 : (t + 1) * 8, :].reshape(64, 128) for t in range(5)]
        c1, c2, c3 = split3(jnp.concatenate(cols, axis=1))
        stack = jnp.concatenate([c1, c1, c1, c2, c2, c3], axis=0)
        o = jnp.dot(pfwd[...], stack, preferred_element_type=F32)
        for t in range(5):
            e = fold(o[:, t * 128 : (t + 1) * 128], lane_low)
            s = jnp.take_along_axis(e, gidx, axis=1) * DISCOUNT
            alive = live[ii * MINE + i * 5 + t].astype(F32)
            s = s + (alive - 1.0) * DEAD
            top = jnp.maximum(top, s)
            sb[pl.ds(pl.multiple_of((i * 5 + t) * 64, 64), 64), :] = s
        return top

    top = lax.fori_loop(0, 5, mix, jnp.full((64, 128), -2 * DEAD, F32))
    for k in range(PLANE):
        msd[k] = top[k * 4 : (k + 1) * 4]
    tops = [
        send(msd.at[g2], mrv.at[slot], sm.at[d + 1], rm.at[d + 1], to)
        for d, (g2, to, _) in enumerate(plane)
    ]
    ownm = local(msd.at[g], mrv.at[slot], 4)
    scat = {}
    owns = {}
    for h in range(NC):
        for k in range(PLANE):
            for t in range(TPC):
                tile = k * 4 + h * TPC + t
                ssend[h, k, t * MINE : (t + 1) * MINE, :] = sb[pl.ds(tile, MINE, stride=64), :]
        scat[h] = [
            send(ssend.at[h, g2], fb.at[h, slot], s2.at[h, d + 1], r2.at[h, d + 1], to)
            for d, (g2, to, _) in enumerate(plane)
        ]
        owns[h] = local(ssend.at[h, g], fb.at[h, slot], 5 + h)

    in3.wait()
    mz[xh] = mass[:, pl.ds(pl.multiple_of(xh * 512, 512), 512)].astype(BF)
    msnd[...] = mass[:, pl.ds(pl.multiple_of((1 - xh) * 512, 512), 512)].astype(BF)
    msend = send(msnd, mz.at[xh], sk.at[1], rk.at[1], across)

    ownm.wait()
    for cp in tops:
        cp.wait_recv()
    mds[...] = jnp.max(mrv[...], axis=0)
    maxes = [
        send(mds, mdr.at[blk], sd.at[d + 1], rd.at[d + 1], to)
        for d, to in enumerate(column)
    ]
    mdr[blk] = mds[...]
    for cp in maxes:
        cp.wait_recv()
    cmax = jnp.max(mdr[...], axis=0)

    ownk.wait()
    for cp in ksend:
        cp.wait_recv()
    for x2 in range(2):
        for b in range(8):
            dst = (b * 2 + x2) * ROWS
            kp[1 - xh, :, dst : dst + ROWS] = kr[x2, b]

    my_rows = pl.ds(pl.multiple_of(blk * 400, 16), 400)

    def rows_of(z_, c_):
        return pl.ds(pl.multiple_of((z_ * 2 + c_) * 400, 16), 400)

    got = {}

    def gather0(n, buf, h):
        ref = buf.at[h, my_rows]
        got[n, h] = [
            send(ref, ref, sg.at[n, h, 0], rg.at[n, h, 0], dev(xh, up, c, ii)),
            send(ref, ref, sg.at[n, h, 1], rg.at[n, h, 1], dev(xh, down, c, ii)),
            send(ref, ref, sg.at[n, h, 2], rg.at[n, h, 2], partner),
        ]

    def gather1(n, buf, h):
        w = got[n, h]
        for k, (src, to) in enumerate(((down, up), (up, down))):
            w[k].wait_recv()
            half = buf.at[h, rows_of(src, c), pl.ds(k * (CW // 2), CW // 2)]
            w.append(send(half, half, sg.at[n, h, 3 + k], rg.at[n, h, 3 + k], dev(xh, to, c, ii)))
            ref = buf.at[h, rows_of(src, c)]
            w.append(send(ref, ref, sg.at[n, h, 5 + k], rg.at[n, h, 5 + k], partner))

    def gather2(n, buf, h):
        w = got[n, h]
        for k, cp in enumerate((w[3], w[5])):
            cp.wait_recv()
            half = buf.at[h, rows_of(far, c), pl.ds(k * (CW // 2), CW // 2)]
            w.append(send(half, half, sg.at[n, h, 7 + k], rg.at[n, h, 7 + k], partner))

    def gather3(n, buf, h):
        w = got[n, h]
        for cp in (w[2], w[4], w[6], w[7], w[8]):
            cp.wait_recv()

    def st_d(h):
        owns[h].wait()
        for cp in scat[h]:
            cp.wait_recv()
        for t in range(TPC):
            for k in range(PLANE):
                fc[k * MINE : (k + 1) * MINE, t * 128 : (t + 1) * 128] = fb[
                    h, k, t * MINE : (t + 1) * MINE, :
                ]
        for t in range(TPC):
            k = h * TPC + t
            lanes = slice(t * 128, (t + 1) * 128)
            dall[h, my_rows, lanes] = jnp.exp(fc[:, lanes] - cmax[k : k + 1, :]).astype(BF)
        gather0(0, dall, h)

    def st_share(h):
        gather3(0, dall, h)
        if h == 0:
            msend.wait_recv()
        for x2 in range(2):
            tots[x2] = jnp.dot(kp[x2], dall[h], preferred_element_type=F32)
        sh = []
        for x2 in range(2):
            sh.append(mz[x2, :, h * CW : (h + 1) * CW].astype(F32) / tots[x2])
        shall[h, my_rows, :] = jnp.concatenate(sh, axis=0).astype(BF)
        gather0(1, shall, h)
        cm = jnp.concatenate([cmax[h * TPC + t : h * TPC + t + 1, :] for t in range(TPC)], axis=1)
        cols = pl.ds(pl.multiple_of(xh * 512 + h * CW, 128), CW)
        vown[h] = cm + jnp.log(tots[xh])
        ownv.append(local(vown.at[h], v_out.at[:, cols], 7 + 2 * NC + h))
        vsend[h] = cm + jnp.log(tots[1 - xh])
        vs.append(send(vsend.at[h], v_out.at[:, cols], sv.at[h], rv.at[h], across))

    vs = []
    ownv = []
    back = {}
    ownb = {}

    def st_move(h):
        gather3(1, shall, h)
        for x2 in range(2):
            tots[x2] = jnp.dot(kp[x2], shall[h], preferred_element_type=F32)
        arrived = jnp.concatenate([tots[0], tots[1]], axis=0)
        for t in range(TPC):
            lanes = slice(t * 128, (t + 1) * 128)
            mv = dall[h, my_rows, lanes].astype(F32) * arrived[:, lanes]
            hi = mv.astype(BF)
            lo = (mv - hi.astype(F32)).astype(BF)
            oh = onehot[h * TPC + t]
            sfr[...] = jnp.dot(hi, oh, preferred_element_type=F32) + jnp.dot(
                lo, oh, preferred_element_type=F32
            )
            for k in range(PLANE):
                csf[k, t * MINE : (t + 1) * MINE, :] = sfr[k * MINE : (k + 1) * MINE, :]
        for k in range(PLANE):
            cs[h, k] = csf[k].astype(BF)
        back[h] = [
            send(cs.at[h, s2_], cr.at[h, g], s3.at[h, d + 1], r3.at[h, d + 1], to)
            for d, (_, to, s2_) in enumerate(plane)
        ]
        ownb[h] = local(cs.at[h, slot], cr.at[h, g], 5 + NC + h)

    stages = [
        st_d,
        lambda h: gather1(0, dall, h),
        lambda h: gather2(0, dall, h),
        st_share,
        lambda h: gather1(1, shall, h),
        lambda h: gather2(1, shall, h),
        st_move,
    ]
    for step in range(NC + len(stages) - 1):
        for s in reversed(range(len(stages))):
            if 0 <= step - s < NC:
                stages[s](step - s)

    for h in range(NC):
        ownb[h].wait()
        for cp in back[h]:
            cp.wait_recv()
        for k in range(PLANE):
            first = k * 4 * MINE + h * PIECE
            xf[first : first + PIECE, :] = cr[h, k].astype(F32)

    @pl.loop(0, 5)
    def _(i):
        x = jnp.concatenate(
            [xf[pl.ds(i * 5 + t, 64, stride=MINE), :] for t in range(5)], axis=1
        ).astype(BF)
        stack = jnp.concatenate([x, x, x, x], axis=0)
        o = jnp.dot(pbwd[...], stack, preferred_element_type=F32)
        for t in range(5):
            e = fold(o[:, t * 128 : (t + 1) * 128], lane_low)
            ns[:, pl.ds(pl.multiple_of(i * 40 + t * 8, 8), 8), :] = e.reshape(8, 8, 128)

    mine = pl.ds(pl.multiple_of(ii * ROWS, 8), ROWS)
    a2a = []
    for d in range(1, INC):
        peer = lax.rem(ii + d, INC)
        a2a.append(send(ns.at[peer], nm_out.at[mine], s4.at[d], r4.at[d], (li, peer)))
    own4 = local(ns.at[ii], nm_out.at[mine], 5 + 2 * NC)
    own4.wait()
    for cp in a2a:
        cp.wait_recv()
    for cp in ownv:
        cp.wait()
    for cp in vs:
        cp.wait_recv()
    for cp in pending:
        cp.wait_send()


def shards(cont_value, flow_util, move_cost, live_mask, trans_weight, asset_policy, mass):
    vm = pl.BlockSpec(memory_space=pltpu.VMEM)
    any_ = pl.BlockSpec(memory_space=pl.ANY)
    dma = pltpu.SemaphoreType.DMA
    v, nm = pl.pallas_call(
        body,
        out_shape=(
            jax.ShapeDtypeStruct((ROWS, 1024), F32),
            jax.ShapeDtypeStruct((8 * ROWS, 128), F32),
        ),
        in_specs=[any_, any_, any_, pl.BlockSpec(memory_space=pltpu.SMEM), vm, vm],
        out_specs=(any_, any_),
        scratch_shapes=[
            pltpu.VMEM((ROWS, 1024), F32),
            pltpu.VMEM((ROWS, L), F32),
            pltpu.VMEM((ROWS, 1024), F32),
            pltpu.VMEM((8, ROWS, ROWS), BF),
            pltpu.VMEM((8, ROWS, ROWS), BF),
            pltpu.VMEM((2, 8, ROWS, ROWS), BF),
            pltpu.VMEM((8 * ROWS, 128), F32),
            pltpu.VMEM((INC, ROWS, 128), F32),
            pltpu.VMEM((MINE * 64, 128), F32),
            pltpu.VMEM((NC, PLANE, PIECE, 128), F32),
            pltpu.VMEM((PLANE, 4, 128), F32),
            pltpu.VMEM((PLANE, 4, 128), F32),
            pltpu.VMEM((4, 128), F32),
            pltpu.VMEM((8, 4, 128), F32),
            pltpu.VMEM((NC, PLANE, PIECE, 128), F32),
            pltpu.VMEM((2 * ROWS, CW), F32),
            pltpu.VMEM((2, ROWS, L), BF),
            pltpu.VMEM((NC, L, CW), BF),
            pltpu.VMEM((NC, L, CW), BF),
            pltpu.VMEM((2, ROWS, 512), BF),
            pltpu.VMEM((ROWS, 512), BF),
            pltpu.VMEM((2, ROWS, CW), F32),
            pltpu.VMEM((NC, ROWS, CW), F32),
            pltpu.VMEM((NC, ROWS, CW), F32),
            pltpu.VMEM((2 * ROWS, 128), F32),
            pltpu.VMEM((PLANE, PIECE, 128), F32),
            pltpu.VMEM((NC, PLANE, PIECE, 128), BF),
            pltpu.VMEM((NC, PLANE, PIECE, 128), BF),
            pltpu.VMEM((MINE * 64, 128), F32),
            pltpu.VMEM((INC, ROWS, 128), F32),
            pltpu.VMEM((64, 128), jnp.int32),
            pltpu.VMEM((128, 128), F32),
            pltpu.VMEM((128, 128), F32),
            pltpu.VMEM((256, 384), BF),
            pltpu.VMEM((256, 256), BF),
            pltpu.VMEM((4, 128, 128), BF),
            dma((7 + 3 * NC,)),
            dma((8,)), dma((8,)), dma((NC, 16)), dma((NC, 16)),
            dma((16,)), dma((16,)), dma((8,)), dma((8,)),
            dma((9,)), dma((9,)), dma((2, NC, 9)), dma((2, NC, 9)),
            dma((NC,)), dma((NC,)), dma((NC, 16)), dma((NC, 16)),
            dma((8,)), dma((8,)),
        ],
        compiler_params=pltpu.CompilerParams(
            collective_id=0, has_side_effects=True, vmem_limit_bytes=60 * 1024 * 1024
        ),
        name="county_step",
    )(cont_value, move_cost, mass, live_mask, trans_weight, asset_policy)
    return flow_util + v, nm.reshape(ROWS, 1024)


def solution(mesh):
    return jax.shard_map(
        shards,
        mesh=mesh,
        in_specs=(
            P("loc", "inc"),
            P("loc", "inc"),
            P("loc", None),
            P("loc"),
            P(),
            P(),
            P("loc", "inc"),
        ),
        out_specs=(P("loc", "inc"), P("loc", "inc")),
        check_vma=False,
    )
```

```python
import jax
import jax.numpy as jnp
from jax import lax
from jax.experimental import pallas as pl
from jax.experimental.pallas import tpu as pltpu
from jax.sharding import PartitionSpec as P

E = 128
A = 64
DISCOUNT = 0.96
DEAD = 1e30

MESH = pl.DeviceIdType.MESH
BF = jnp.bfloat16
F32 = jnp.float32

ROWS = 200
INC = 8
MINE = ROWS // INC
PLANE = 16
L = 3200
NC = 2
TPC = 4 // NC
CW = TPC * 128
PIECE = TPC * MINE


def fold(o, lane_low):
    direct = jnp.where(lane_low, o[0:64], o[192:256])
    cross = jnp.where(lane_low, o[128:192], o[64:128])
    return direct + pltpu.roll(cross, 64, axis=1)


def split3(x):
    a = x.astype(BF)
    r = x - a.astype(F32)
    b = r.astype(BF)
    c = (r - b.astype(F32)).astype(BF)
    return a, b, c


def body(
    cont_h, mc_h, mass_h, live, tw, pol,
    v_out, nm_out,
    cont, mc, mass,
    ko, kt, kr, abuf, rbuf, sb, ssend, msd, mrv, mds, mdr, fb, fc, kp, dall, shall, mz, msnd,
    tots, vown, vsend, sfr, csf, cs, cr, xf, ns,
    psc, gsc, pscr, ptscr, pfwd, pbwd, onehot,
    lsem, s1, r1, s2, r2, sm, rm, sd, rd, sk, rk, sg, rg, sv, rv, s3, r3, s4, r4,
):
    li = lax.axis_index("loc")
    ii = lax.axis_index("inc")
    xh = li // 8
    z = lax.rem(li // 2, 4)
    c = lax.rem(li, 2)
    g = ii * 2 + xh
    slot = xh * 8 + ii
    blk = z * 2 + c

    def dev(xh_, z_, c_, ii_):
        return ((xh_ * 4 + z_) * 2 + c_, ii_)

    up = lax.rem(z + 1, 4)
    down = lax.rem(z + 3, 4)
    far = lax.rem(z + 2, 4)
    partner = dev(xh, z, 1 - c, ii)
    across = dev(1 - xh, z, c, ii)
    pending = []

    def send(src, dst, ssem, rsem, to):
        cp = pltpu.make_async_remote_copy(
            src_ref=src, dst_ref=dst, send_sem=ssem, recv_sem=rsem,
            device_id=to, device_id_type=MESH,
        )
        cp.start()
        pending.append(cp)
        return cp

    def local(src, dst, k):
        cp = pltpu.make_async_copy(src, dst, lsem.at[k])
        cp.start()
        return cp

    in1 = local(cont_h, cont, 0)
    in2 = local(mc_h, mc, 1)
    in3 = local(mass_h, mass, 2)

    barrier = pltpu.get_barrier_semaphore()
    plane = []
    for d in range(1, PLANE):
        g2 = lax.rem(g + d, PLANE)
        plane.append((g2, dev(lax.rem(g2, 2), z, c, g2 // 2), lax.rem(g2, 2) * 8 + g2 // 2))
    column = []
    for d in range(1, 8):
        b2 = lax.rem(blk + d, 8)
        column.append(dev(xh, b2 // 2, lax.rem(b2, 2), ii))
    for _, to, _ in plane:
        pl.semaphore_signal(barrier, inc=1, device_id=to, device_id_type=MESH)
    for to in column:
        pl.semaphore_signal(barrier, inc=1, device_id=to, device_id_type=MESH)

    in1.wait()
    for k in range(8):
        abuf[pl.ds(k, ROWS, stride=8), :] = cont[:, k * 128 : (k + 1) * 128]
    in2.wait()
    for x2 in range(2):

        @pl.when(xh == x2)
        def _():
            for b in range(8):
                src = (x2 * 8 + b) * ROWS
                ko[b] = jnp.exp(-mc[:, src : src + ROWS]).astype(BF)

    pl.semaphore_wait(barrier, PLANE - 1 + 7)
    beside = dev(1 - xh, z, c, ii + 1 - 2 * lax.rem(ii, 2))
    y = ii // 2
    part = pl.ds(y * 2, 2)
    kfirst = send(ko.at[part], kr.at[xh, part], sk.at[0], rk.at[0], beside)
    ksend = []

    a2a = []
    for d in range(1, INC):
        peer = lax.rem(ii + d, INC)
        a2a.append(send(
            abuf.at[pl.ds(pl.multiple_of(peer * ROWS, 8), ROWS)], rbuf.at[ii],
            s1.at[d], r1.at[d], (li, peer),
        ))
    own1 = local(abuf.at[pl.ds(pl.multiple_of(ii * ROWS, 8), ROWS)], rbuf.at[ii], 3)

    for x2 in range(2):
        for b in range(8):
            src = (x2 * 8 + b) * ROWS
            dst = (b * 2 + x2) * ROWS
            kp[xh, :, dst : dst + ROWS] = jnp.exp(-mc[:, src : src + ROWS]).astype(BF)

        @pl.when(xh != x2)
        def _():
            for b in range(8):
                src = (x2 * 8 + b) * ROWS
                kt[b] = jnp.exp(-mc[:, src : src + ROWS]).T.astype(BF)

    for d, to in enumerate(column):
        b2 = lax.rem(blk + d + 1, 8)
        ksend.append(send(kt.at[b2], kr.at[xh, blk], sk.at[2 + d], rk.at[2 + d], to))
    ownk = local(kt.at[blk], kr.at[xh, blk], 6 + 2 * NC)

    row = lax.broadcasted_iota(jnp.int32, (128, 128), 0)
    col = lax.broadcasted_iota(jnp.int32, (128, 128), 1)
    raised = tw[...] + jnp.where(row == col, 16.0, 0.0)
    prob = raised / jnp.sum(raised, axis=1, keepdims=True)
    pscr[...] = prob
    ptscr[...] = prob.T

    def pick(parity, high):
        want = col - 64 if high else col
        keep = (want >= 0) & (want < 64) & (row == 2 * want + parity)
        return jnp.where(keep, 1.0, 0.0).astype(BF)

    for scr, out, pairs in (
        (pscr, pfwd, ((0, 1), (2, 0), (1, 0))),
        (ptscr, pbwd, ((0, 1), (2, None))),
    ):
        for po in range(2):
            parts = split3(scr[pl.ds(po, 64, stride=2), :])
            for pi in range(2):
                low, high = pick(pi, False), pick(pi, True)
                for n, (a, b) in enumerate(pairs):
                    q = jnp.dot(parts[a], low, preferred_element_type=F32)
                    if b is not None:
                        q = q + jnp.dot(parts[b], high, preferred_element_type=F32)
                    r0 = (po * 2 + pi) * 64
                    out[r0 : r0 + 64, n * 128 : (n + 1) * 128] = q.astype(BF)

    lane64 = lax.broadcasted_iota(jnp.int32, (64, 128), 1)
    lane_low = lane64 < 64
    tall = jnp.concatenate([pol[...].astype(F32), jnp.zeros((64, 128), F32)], axis=0)
    psc[...] = tall.T
    odd = pltpu.roll(psc[pl.ds(1, 64, stride=2), :] + 64.0, 64, axis=1)
    gsc[...] = jnp.where(lane_low, psc[pl.ds(0, 64, stride=2), :], odd).astype(jnp.int32)
    gidx = gsc[...]
    gown = gsc[pl.ds(g * 4, 4), :]
    for t in range(4):
        wide = jnp.broadcast_to(gown[t : t + 1].astype(F32), (128, 128)).T
        onehot[t] = jnp.where(wide == col.astype(F32), 1.0, 0.0).astype(BF)

    own1.wait()
    for cp in a2a:
        cp.wait_recv()

    def mix(i, top):
        base = pl.multiple_of(i * 40, 8)
        piece = rbuf[:, pl.ds(base, 40), :]
        cols = [piece[:, t * 8 : (t + 1) * 8, :].reshape(64, 128) for t in range(5)]
        c1, c2, c3 = split3(jnp.concatenate(cols, axis=1))
        stack = jnp.concatenate([c1, c1, c1, c2, c2, c3], axis=0)
        o = jnp.dot(pfwd[...], stack, preferred_element_type=F32)
        for t in range(5):
            e = fold(o[:, t * 128 : (t + 1) * 128], lane_low)
            s = jnp.take_along_axis(e, gidx, axis=1) * DISCOUNT
            alive = live[ii * MINE + i * 5 + t].astype(F32)
            s = s + (alive - 1.0) * DEAD
            top = jnp.maximum(top, s)
            sb[pl.ds(pl.multiple_of((i * 5 + t) * 64, 64), 64), :] = s
        return top

    top = lax.fori_loop(0, 5, mix, jnp.full((64, 128), -2 * DEAD, F32))
    for k in range(PLANE):
        msd[k] = top[k * 4 : (k + 1) * 4]
    tops = [
        send(msd.at[g2], mrv.at[slot], sm.at[d + 1], rm.at[d + 1], to)
        for d, (g2, to, _) in enumerate(plane)
    ]
    ownm = local(msd.at[g], mrv.at[slot], 4)
    scat = {}
    owns = {}
    for h in range(NC):
        for k in range(PLANE):
            for t in range(TPC):
                tile = k * 4 + h * TPC + t
                ssend[h, k, t * MINE : (t + 1) * MINE, :] = sb[pl.ds(tile, MINE, stride=64), :]
        scat[h] = [
            send(ssend.at[h, g2], fb.at[h, slot], s2.at[h, d + 1], r2.at[h, d + 1], to)
            for d, (g2, to, _) in enumerate(plane)
        ]
        owns[h] = local(ssend.at[h, g], fb.at[h, slot], 5 + h)

    kfirst.wait_recv()
    for d in (2, 1, 3):
        ref = kr.at[1 - xh, part]
        to = dev(xh, z, c, lax.rem(ii + 2 * d, INC))
        ksend.append(send(ref, ref, sk.at[8 + d], rk.at[8 + d], to))

    in3.wait()
    mz[xh] = mass[:, pl.ds(pl.multiple_of(xh * 512, 512), 512)].astype(BF)
    msnd[...] = mass[:, pl.ds(pl.multiple_of((1 - xh) * 512, 512), 512)].astype(BF)
    msend = send(msnd, mz.at[xh], sk.at[1], rk.at[1], across)

    ownm.wait()
    for cp in tops:
        cp.wait_recv()
    mds[...] = jnp.max(mrv[...], axis=0)
    maxes = [
        send(mds, mdr.at[blk], sd.at[d + 1], rd.at[d + 1], to)
        for d, to in enumerate(column)
    ]
    mdr[blk] = mds[...]
    for cp in maxes:
        cp.wait_recv()
    cmax = jnp.max(mdr[...], axis=0)

    my_rows = pl.ds(pl.multiple_of(blk * 400, 16), 400)

    def rows_of(z_, c_):
        return pl.ds(pl.multiple_of((z_ * 2 + c_) * 400, 16), 400)

    got = {}

    def gather0(n, buf, h):
        ref = buf.at[h, my_rows]
        got[n, h] = [
            send(ref, ref, sg.at[n, h, 0], rg.at[n, h, 0], dev(xh, up, c, ii)),
            send(ref, ref, sg.at[n, h, 1], rg.at[n, h, 1], dev(xh, down, c, ii)),
            send(ref, ref, sg.at[n, h, 2], rg.at[n, h, 2], partner),
        ]

    def gather1(n, buf, h):
        w = got[n, h]
        for k, (src, to) in enumerate(((down, up), (up, down))):
            w[k].wait_recv()
            half = buf.at[h, rows_of(src, c), pl.ds(k * (CW // 2), CW // 2)]
            w.append(send(half, half, sg.at[n, h, 3 + k], rg.at[n, h, 3 + k], dev(xh, to, c, ii)))
            ref = buf.at[h, rows_of(src, c)]
            w.append(send(ref, ref, sg.at[n, h, 5 + k], rg.at[n, h, 5 + k], partner))

    def gather2(n, buf, h):
        w = got[n, h]
        for k, cp in enumerate((w[3], w[5])):
            cp.wait_recv()
            half = buf.at[h, rows_of(far, c), pl.ds(k * (CW // 2), CW // 2)]
            w.append(send(half, half, sg.at[n, h, 7 + k], rg.at[n, h, 7 + k], partner))

    def gather3(n, buf, h):
        w = got[n, h]
        for cp in (w[2], w[4], w[6], w[7], w[8]):
            cp.wait_recv()

    def st_d(h):
        owns[h].wait()
        for cp in scat[h]:
            cp.wait_recv()
        for t in range(TPC):
            for k in range(PLANE):
                fc[k * MINE : (k + 1) * MINE, t * 128 : (t + 1) * 128] = fb[
                    h, k, t * MINE : (t + 1) * MINE, :
                ]
        for t in range(TPC):
            k = h * TPC + t
            lanes = slice(t * 128, (t + 1) * 128)
            dall[h, my_rows, lanes] = jnp.exp(fc[:, lanes] - cmax[k : k + 1, :]).astype(BF)
        gather0(0, dall, h)

    def take_kernel(h):
        if h > 0:
            return
        ownk.wait()
        for cp in ksend:
            cp.wait_recv()
        for x2 in range(2):
            for b in range(8):
                dst = (b * 2 + x2) * ROWS
                kp[1 - xh, :, dst : dst + ROWS] = kr[x2, b]
        msend.wait_recv()

    def st_share(h):
        take_kernel(h)
        gather3(0, dall, h)
        for x2 in range(2):
            tots[x2] = jnp.dot(kp[x2], dall[h], preferred_element_type=F32)
        sh = []
        for x2 in range(2):
            sh.append(mz[x2, :, h * CW : (h + 1) * CW].astype(F32) / tots[x2])
        shall[h, my_rows, :] = jnp.concatenate(sh, axis=0).astype(BF)
        gather0(1, shall, h)
        cm = jnp.concatenate([cmax[h * TPC + t : h * TPC + t + 1, :] for t in range(TPC)], axis=1)
        cols = pl.ds(pl.multiple_of(xh * 512 + h * CW, 128), CW)
        vown[h] = cm + jnp.log(tots[xh])
        ownv.append(local(vown.at[h], v_out.at[:, cols], 7 + 2 * NC + h))
        vsend[h] = cm + jnp.log(tots[1 - xh])
        vs.append(send(vsend.at[h], v_out.at[:, cols], sv.at[h], rv.at[h], across))

    vs = []
    ownv = []
    back = {}
    ownb = {}

    def st_move(h):
        gather3(1, shall, h)
        for x2 in range(2):
            tots[x2] = jnp.dot(kp[x2], shall[h], preferred_element_type=F32)
        arrived = jnp.concatenate([tots[0], tots[1]], axis=0)
        for t in range(TPC):
            lanes = slice(t * 128, (t + 1) * 128)
            mv = dall[h, my_rows, lanes].astype(F32) * arrived[:, lanes]
            hi = mv.astype(BF)
            lo = (mv - hi.astype(F32)).astype(BF)
            oh = onehot[h * TPC + t]
            sfr[...] = jnp.dot(hi, oh, preferred_element_type=F32) + jnp.dot(
                lo, oh, preferred_element_type=F32
            )
            for k in range(PLANE):
                csf[k, t * MINE : (t + 1) * MINE, :] = sfr[k * MINE : (k + 1) * MINE, :]
        for k in range(PLANE):
            cs[h, k] = csf[k].astype(BF)
        back[h] = [
            send(cs.at[h, s2_], cr.at[h, g], s3.at[h, d + 1], r3.at[h, d + 1], to)
            for d, (_, to, s2_) in enumerate(plane)
        ]
        ownb[h] = local(cs.at[h, slot], cr.at[h, g], 5 + NC + h)

    stages = [
        st_d,
        lambda h: gather1(0, dall, h),
        lambda h: gather2(0, dall, h),
        st_share,
        lambda h: gather1(1, shall, h),
        lambda h: gather2(1, shall, h),
        st_move,
    ]
    for step in range(NC + len(stages) - 1):
        for s in reversed(range(len(stages))):
            if 0 <= step - s < NC:
                stages[s](step - s)

    for h in range(NC):
        ownb[h].wait()
        for cp in back[h]:
            cp.wait_recv()
        for k in range(PLANE):
            first = k * 4 * MINE + h * PIECE
            xf[first : first + PIECE, :] = cr[h, k].astype(F32)

    a2a = []
    for i in range(5):
        x = jnp.concatenate(
            [xf[pl.ds(i * 5 + t, 64, stride=MINE), :] for t in range(5)], axis=1
        ).astype(BF)
        stack = jnp.concatenate([x, x, x, x], axis=0)
        o = jnp.dot(pbwd[...], stack, preferred_element_type=F32)
        for t in range(5):
            e = fold(o[:, t * 128 : (t + 1) * 128], lane_low)
            ns[:, i * 40 + t * 8 : i * 40 + t * 8 + 8, :] = e.reshape(8, 8, 128)
        there = pl.ds(pl.multiple_of(ii * ROWS + i * 40, 8), 40)
        for d in range(1, INC):
            peer = lax.rem(ii + d, INC)
            a2a.append(send(
                ns.at[peer, pl.ds(i * 40, 40)], nm_out.at[there],
                s4.at[i, d], r4.at[i, d], (li, peer),
            ))
    mine = pl.ds(pl.multiple_of(ii * ROWS, 8), ROWS)
    own4 = local(ns.at[ii], nm_out.at[mine], 5 + 2 * NC)
    own4.wait()
    for cp in a2a:
        cp.wait_recv()
    for cp in ownv:
        cp.wait()
    for cp in vs:
        cp.wait_recv()
    for cp in pending:
        cp.wait_send()


def shards(cont_value, flow_util, move_cost, live_mask, trans_weight, asset_policy, mass):
    vm = pl.BlockSpec(memory_space=pltpu.VMEM)
    any_ = pl.BlockSpec(memory_space=pl.ANY)
    dma = pltpu.SemaphoreType.DMA
    v, nm = pl.pallas_call(
        body,
        out_shape=(
            jax.ShapeDtypeStruct((ROWS, 1024), F32),
            jax.ShapeDtypeStruct((8 * ROWS, 128), F32),
        ),
        in_specs=[any_, any_, any_, pl.BlockSpec(memory_space=pltpu.SMEM), vm, vm],
        out_specs=(any_, any_),
        scratch_shapes=[
            pltpu.VMEM((ROWS, 1024), F32),
            pltpu.VMEM((ROWS, L), F32),
            pltpu.VMEM((ROWS, 1024), F32),
            pltpu.VMEM((8, ROWS, ROWS), BF),
            pltpu.VMEM((8, ROWS, ROWS), BF),
            pltpu.VMEM((2, 8, ROWS, ROWS), BF),
            pltpu.VMEM((8 * ROWS, 128), F32),
            pltpu.VMEM((INC, ROWS, 128), F32),
            pltpu.VMEM((MINE * 64, 128), F32),
            pltpu.VMEM((NC, PLANE, PIECE, 128), F32),
            pltpu.VMEM((PLANE, 4, 128), F32),
            pltpu.VMEM((PLANE, 4, 128), F32),
            pltpu.VMEM((4, 128), F32),
            pltpu.VMEM((8, 4, 128), F32),
            pltpu.VMEM((NC, PLANE, PIECE, 128), F32),
            pltpu.VMEM((2 * ROWS, CW), F32),
            pltpu.VMEM((2, ROWS, L), BF),
            pltpu.VMEM((NC, L, CW), BF),
            pltpu.VMEM((NC, L, CW), BF),
            pltpu.VMEM((2, ROWS, 512), BF),
            pltpu.VMEM((ROWS, 512), BF),
            pltpu.VMEM((2, ROWS, CW), F32),
            pltpu.VMEM((NC, ROWS, CW), F32),
            pltpu.VMEM((NC, ROWS, CW), F32),
            pltpu.VMEM((2 * ROWS, 128), F32),
            pltpu.VMEM((PLANE, PIECE, 128), F32),
            pltpu.VMEM((NC, PLANE, PIECE, 128), BF),
            pltpu.VMEM((NC, PLANE, PIECE, 128), BF),
            pltpu.VMEM((MINE * 64, 128), F32),
            pltpu.VMEM((INC, ROWS, 128), F32),
            pltpu.VMEM((128, 128), F32),
            pltpu.VMEM((64, 128), jnp.int32),
            pltpu.VMEM((128, 128), F32),
            pltpu.VMEM((128, 128), F32),
            pltpu.VMEM((256, 384), BF),
            pltpu.VMEM((256, 256), BF),
            pltpu.VMEM((4, 128, 128), BF),
            dma((7 + 3 * NC,)),
            dma((8,)), dma((8,)), dma((NC, 16)), dma((NC, 16)),
            dma((16,)), dma((16,)), dma((8,)), dma((8,)),
            dma((12,)), dma((12,)), dma((2, NC, 9)), dma((2, NC, 9)),
            dma((NC,)), dma((NC,)), dma((NC, 16)), dma((NC, 16)),
            dma((5, 8)), dma((5, 8)),
        ],
        compiler_params=pltpu.CompilerParams(
            collective_id=0, has_side_effects=True, vmem_limit_bytes=60 * 1024 * 1024
        ),
        name="county_step",
    )(cont_value, move_cost, mass, live_mask, trans_weight, asset_policy.T)
    return flow_util + v, nm.reshape(ROWS, 1024)


def solution(mesh):
    return jax.shard_map(
        shards,
        mesh=mesh,
        in_specs=(
            P("loc", "inc"),
            P("loc", "inc"),
            P("loc", None),
            P("loc"),
            P(),
            P(),
            P("loc", "inc"),
        ),
        out_specs=(P("loc", "inc"), P("loc", "inc")),
        check_vma=False,
    )
```
